256 devices in a mesh: frame: 32 (over y, x, core), space: 8 (over z).
Axes of the slice: x: 4, y: 4, z: 8, core: 2. Of those that a mesh axis runs over, the one named last changes fastest.
Arguments:
- query_tokens: bfloat16 [32, 2048, 2240], P('frame', 'space'), may hold values from -6 to 6
- key_tokens: bfloat16 [32, 2048, 2240], P('frame', 'space'), may hold values from -500 to 500
- value_tokens: bfloat16 [32, 2048, 2240], P('frame', 'space'), may hold values from -6 to 6
- out_grad: bfloat16 [32, 2048, 2240], P('frame', 'space'), may hold values from -768 to 768
Outputs:
- query_grad: float32 [32, 2048, 2240], P('frame', 'space')
- key_grad: float32 [32, 2048, 2240], P('frame', 'space')
- value_grad: float32 [32, 2048, 2240], P('frame', 'space')
The draws below stay inside these ranges and needn't reach their ends.
All inputs are finite; a program needn't handle non-finite values.
Results may differ from the reference program's by a relative error of at most 0.0041.
Values sent between devices are 32-bit elements; how exact they have to be, the bound alone decides.
No kernel may reach another device: no remote copies, remote signals or barrier semaphores. Data moves between devices by JAX's collectives and lax.ppermute only.
A program may use at most 128 MiB of HBM per device.

```python
import math
import jax
import jax.numpy as jnp
from jax import lax

HEADS = 20
HEAD_DIM = 112
WIDTH = 2240
SPACE_TOK = 2048
BLOCKS = 32


def draw_key_tokens(key, part):
    first, second, third = jax.random.split(key, 3)
    rows = jnp.exp(jax.random.uniform(second, (BLOCKS, SPACE_TOK, 1), minval=0.0, maxval=math.log(10.0)))
    columns = jnp.exp(jax.random.uniform(third, (WIDTH,), minval=0.0, maxval=math.log(10.0)))
    base = jnp.clip(jax.random.normal(first, (BLOCKS, SPACE_TOK, WIDTH)), -4.0, 4.0)
    result = base * rows * columns[None, None, :]
    return result.astype(jnp.bfloat16)


def level_of(stream_key, extent, shards, least, top_value):
    def one(dim, parts):
        steps = jax.random.uniform(jax.random.fold_in(jax.random.fold_in(stream_key, 6), dim), (parts,), jnp.float32, least / len(shards), top_value / len(shards))
        return jnp.repeat(jnp.exp(steps), extent[dim] // parts).reshape((-1,) + (1,) * (len(extent) - dim - 1))

    loudness = one(*shards[0])
    for cut in shards[1:]:
        loudness = loudness * one(*cut)
    return loudness


def scatter_about(key, extent, scale, reach, cuts=(), kind=jnp.bfloat16):
    level = level_of(key, extent, cuts, -0.22, 0.18) if cuts else 1.0
    values = jax.random.normal(key, extent, jnp.float32) * scale * level
    return jnp.minimum(jnp.maximum(values, -reach), reach).astype(kind)


def setup_inputs(seed: int = 0) -> dict:
    seeds = jax.random.split(jax.random.key(seed), 5)
    query_tokens = scatter_about(seeds[0], (BLOCKS, SPACE_TOK, WIDTH), 1.0, 6.0, ((0, 32), (1, 8)))
    key_tokens = draw_key_tokens(jax.random.fold_in(seeds[4], 71), 0)
    value_tokens = scatter_about(seeds[2], (BLOCKS, SPACE_TOK, WIDTH), 1.0, 6.0, ((0, 32), (1, 8)))
    out_grad = scatter_about(seeds[3], (BLOCKS, SPACE_TOK, WIDTH), 128.0, 768.0, ((0, 32), (1, 8)))
    return dict(query_tokens=query_tokens, key_tokens=key_tokens, value_tokens=value_tokens, out_grad=out_grad)


HIGH = lax.Precision.HIGHEST


def block_state(block):
    key_block, value_block = block
    k_feat = jnp.maximum(key_block, 0).astype(jnp.float32).reshape(SPACE_TOK, HEADS, HEAD_DIM)
    v_heads = value_block.astype(jnp.float32).reshape(SPACE_TOK, HEADS, HEAD_DIM)
    local_state = jnp.einsum("thi,thj->ihj", k_feat, v_heads, precision=HIGH)
    local_z = jnp.sum(k_feat, axis=0).T
    return local_state, local_z


def query_phase(block):
    query_block, grad_block, state, zsum = block
    q_heads = query_block.reshape(SPACE_TOK, HEADS, HEAD_DIM)
    q_feat = jnp.maximum(q_heads, 0).astype(jnp.float32)
    out_heads = grad_block.astype(jnp.float32).reshape(SPACE_TOK, HEADS, HEAD_DIM)
    numerator = jnp.einsum("thi,ihj->thj", q_feat, state, precision=HIGH)
    denominator = jnp.einsum("thi,ih->th", q_feat, zsum, precision=HIGH) + 1.0
    scaled = (out_heads / denominator[:, :, None]).astype(jnp.bfloat16)
    scaled = lax.optimization_barrier(scaled).astype(jnp.float32)
    denom_grad = -jnp.sum(out_heads * numerator, axis=-1) / (denominator * denominator)
    direct = jnp.einsum("thj,ihj->thi", scaled, state, precision=HIGH)
    query_grad = jnp.where(q_heads > 0, direct + denom_grad[:, :, None] * zsum.T[None], 0.0)
    local_grad = jnp.einsum("thi,thj->ihj", q_feat, scaled, precision=HIGH)
    local_zgrad = jnp.einsum("thi,th->ih", q_feat, denom_grad, precision=HIGH)
    return query_grad.reshape(SPACE_TOK, WIDTH), local_grad, local_zgrad


def key_phase(block):
    key_block, value_block, state_grad, zsum_grad = block
    k_heads = key_block.reshape(SPACE_TOK, HEADS, HEAD_DIM)
    k_feat = jnp.maximum(k_heads, 0).astype(jnp.float32)
    v_heads = value_block.astype(jnp.float32).reshape(SPACE_TOK, HEADS, HEAD_DIM)
    value_grad = jnp.einsum("thi,ihj->thj", k_feat, state_grad, precision=HIGH)
    key_part = jnp.einsum("thj,ihj->thi", v_heads, state_grad, precision=HIGH)
    key_grad = jnp.where(k_heads > 0, key_part + zsum_grad.T[None], 0.0)
    return key_grad.reshape(SPACE_TOK, WIDTH), value_grad.reshape(SPACE_TOK, WIDTH)


def reference(query_tokens, key_tokens, value_tokens, out_grad):
    local_state, local_z = lax.map(block_state, (key_tokens, value_tokens))
    state = jnp.cumsum(local_state, axis=0)
    zsum = jnp.cumsum(local_z, axis=0)
    query_grad, local_grad, local_zgrad = lax.map(query_phase, (query_tokens, out_grad, state, zsum))
    state_grad = jnp.flip(jnp.cumsum(jnp.flip(local_grad, 0), axis=0), 0)
    zsum_grad = jnp.flip(jnp.cumsum(jnp.flip(local_zgrad, 0), axis=0), 0)
    key_grad, value_grad = lax.map(key_phase, (key_tokens, value_tokens, state_grad, zsum_grad))
    return query_grad, key_grad, value_grad
```

```python
import jax
import jax.numpy as jnp
from jax import lax
from jax.experimental import pallas as pl
from jax.experimental.pallas import tpu as pltpu
from jax.sharding import PartitionSpec as P

HEADS = 20
HEAD_DIM = 112
WIDTH = HEADS * HEAD_DIM
LANES = 128
ROWS = HEADS * HEAD_DIM
FRAMES = 32
SPACES = 8
TOK = 128
VMEM_LIMIT = 48 * 1024 * 1024
NN = (((1,), (0,)), ((), ()))
NT = (((1,), (1,)), ((), ()))
TN = (((0,), (0,)), ((), ()))


def mm(a, b, dims):
    return lax.dot_general(a, b, dims, preferred_element_type=jnp.float32)


def split(x):
    high = x.astype(jnp.bfloat16)
    return high, (x - high.astype(jnp.float32)).astype(jnp.bfloat16)


def head(h):
    return slice(h * HEAD_DIM, (h + 1) * HEAD_DIM)


def relu(x):
    return jnp.maximum(x, jnp.zeros_like(x))


def put_state(ref, h, value, first):
    wide = jnp.concatenate([value, jnp.zeros((HEAD_DIM, LANES - HEAD_DIM), jnp.float32)], axis=1)

    @pl.when(first)
    def _():
        ref[head(h), :] = wide

    @pl.when(jnp.logical_not(first))
    def _():
        ref[head(h), :] += wide


def state_kernel(k_ref, v_ref, state_ref, z_ref):
    first = pl.program_id(0) == 0
    total = jnp.sum(relu(k_ref[...]).astype(jnp.float32), axis=0, keepdims=True)

    @pl.when(first)
    def _():
        z_ref[...] = total

    @pl.when(jnp.logical_not(first))
    def _():
        z_ref[...] += total

    for h in range(HEADS):
        put_state(state_ref, h, mm(relu(k_ref[:, head(h)]), v_ref[:, head(h)], TN), first)


def denominators(q, z_row):
    z_wide = jnp.broadcast_to(z_row, (HEAD_DIM, HEAD_DIM))
    high, low = split(z_wide)
    return mm(q, high, NT) + mm(q, low, NT) + 1.0


def grad_kernel(q_ref, g_ref, z_ref, grad_ref):
    first = pl.program_id(0) == 0
    for h in range(HEADS):
        q = relu(q_ref[:, head(h)])
        scaled = (g_ref[:, head(h)].astype(jnp.float32) / denominators(q, z_ref[:, head(h)])).astype(jnp.bfloat16)
        put_state(grad_ref, h, mm(q, scaled, TN), first)


def query_kernel(q_ref, g_ref, z_ref, s_ref, out_ref, zgrad_ref):
    first = pl.program_id(0) == 0
    for h in range(HEADS):
        q_raw = q_ref[:, head(h)]
        q = relu(q_raw)
        z_row = z_ref[:, head(h)]
        wide = g_ref[:, head(h)].astype(jnp.float32)
        denominator = denominators(q, z_row)
        scaled = (wide / denominator).astype(jnp.bfloat16)
        high, low = split(s_ref[head(h), :HEAD_DIM])
        numerator = mm(q, high, NN) + mm(q, low, NN)
        total = jnp.sum(wide * numerator, axis=1, keepdims=True)
        denom_grad = -total / (denominator * denominator)
        direct = mm(scaled, high, NT) + mm(scaled, low, NT)
        out_ref[:, head(h)] = jnp.where(q_raw > 0, direct + denom_grad * z_row, 0.0)
        part = jnp.sum(q.astype(jnp.float32) * denom_grad, axis=0, keepdims=True)

        @pl.when(first)
        def _():
            zgrad_ref[:, head(h)] = part

        @pl.when(jnp.logical_not(first))
        def _():
            zgrad_ref[:, head(h)] += part


def key_kernel(k_ref, v_ref, sg_ref, zg_ref, key_ref, value_ref):
    for h in range(HEADS):
        k_raw = k_ref[:, head(h)]
        k = relu(k_raw)
        high, low = split(sg_ref[head(h), :HEAD_DIM])
        value_ref[:, head(h)] = mm(k, high, NN) + mm(k, low, NN)
        v = v_ref[:, head(h)]
        part = mm(v, high, NT) + mm(v, low, NT)
        key_ref[:, head(h)] = jnp.where(k_raw > 0, part + zg_ref[:, head(h)], 0.0)


TOKEN_BLOCK = pl.BlockSpec((TOK, WIDTH), lambda t: (t, 0))
STATE_BLOCK = pl.BlockSpec((ROWS, LANES), lambda t: (0, 0))
ROW_BLOCK = pl.BlockSpec((1, WIDTH), lambda t: (0, 0))
STATE_SHAPE = jax.ShapeDtypeStruct((ROWS, LANES), jnp.float32)
ROW_SHAPE = jax.ShapeDtypeStruct((1, WIDTH), jnp.float32)


def call(kernel, name, tokens, in_specs, out_specs, out_shape, flops, size):
    return pl.pallas_call(
        kernel,
        grid=(tokens // TOK,),
        in_specs=in_specs,
        out_specs=out_specs,
        out_shape=out_shape,
        name=name,
        compiler_params=pltpu.CompilerParams(vmem_limit_bytes=VMEM_LIMIT),
        cost_estimate=pl.CostEstimate(flops=flops, bytes_accessed=size, transcendentals=0),
    )


def spread(row, axis, devices):
    every = jnp.broadcast_to(row.reshape(1, 1, WIDTH), (devices, 1, WIDTH))
    return lax.all_to_all(every, axis, 0, 0, tiled=True)


def small_scan(row, reverse):
    total = jnp.sum(spread(row, "space", SPACES), axis=0)
    every = spread(total, "frame", FRAMES)
    here = lax.axis_index("frame")
    frames = lax.broadcasted_iota(jnp.int32, (FRAMES, 1, 1), 0)
    wanted = frames >= here if reverse else frames <= here
    return jnp.sum(jnp.where(wanted, every, 0.0), axis=0)


def piece_scans(state_piece, grad_piece):
    rows = state_piece.shape[0]
    padded = 9 * FRAMES
    both = jnp.stack([state_piece, grad_piece])
    both = jnp.pad(both, ((0, 0), (0, padded - rows), (0, 0)))
    slots = both.reshape(2, FRAMES, 9, LANES).transpose(1, 0, 2, 3).reshape(FRAMES, 18, LANES)
    slots = lax.all_to_all(slots, "frame", 0, 0, tiled=True)
    forward = jnp.cumsum(slots[:, :9], axis=0)
    backward = lax.cumsum(slots[:, 9:], axis=0, reverse=True)
    slots = jnp.concatenate([forward, backward], axis=1)
    slots = lax.all_to_all(slots, "frame", 0, 0, tiled=True)
    both = slots.reshape(FRAMES, 2, 9, LANES).transpose(1, 0, 2, 3).reshape(2, padded, LANES)
    return both[0, :rows], both[1, :rows]


def gather_pieces(piece):
    every = jnp.broadcast_to(piece[None], (SPACES,) + piece.shape)
    return lax.all_to_all(every, "space", 0, 0, tiled=True).reshape(ROWS, LANES)


def reduce_pieces(state):
    pieces = state.reshape(SPACES, ROWS // SPACES, LANES)
    return jnp.sum(lax.all_to_all(pieces, "space", 0, 0, tiled=True), axis=0)


def on_device(query_tokens, key_tokens, value_tokens, out_grad):
    tokens = query_tokens.shape[1]
    q, k, v, g = (a.reshape(tokens, WIDTH) for a in (query_tokens, key_tokens, value_tokens, out_grad))
    work = 2 * tokens * WIDTH * HEAD_DIM
    part = tokens * WIDTH * 2
    whole = ROWS * LANES * 4
    local_state, local_z = call(
        state_kernel, "local_state", tokens, [TOKEN_BLOCK] * 2, [STATE_BLOCK, ROW_BLOCK],
        [STATE_SHAPE, ROW_SHAPE], work, 2 * part + whole,
    )(k, v)
    state_piece = lax.psum_scatter(local_state, "space", scatter_dimension=0, tiled=True)
    zsum = small_scan(local_z, False)
    local_grad = call(
        grad_kernel, "local_grad", tokens, [TOKEN_BLOCK] * 2 + [ROW_BLOCK], STATE_BLOCK,
        STATE_SHAPE, 3 * work, 2 * part + whole,
    )(q, g, zsum)
    grad_piece = reduce_pieces(local_grad)
    state_piece, grad_piece = piece_scans(state_piece, grad_piece)
    state = gather_pieces(state_piece)
    state_grad = lax.all_gather(grad_piece, "space", axis=0, tiled=True)
    token_out = jax.ShapeDtypeStruct((tokens, WIDTH), jnp.float32)
    query_grad, local_zgrad = call(
        query_kernel, "query_grad", tokens, [TOKEN_BLOCK] * 2 + [ROW_BLOCK, STATE_BLOCK],
        [TOKEN_BLOCK, ROW_BLOCK], [token_out, ROW_SHAPE], 6 * work, 4 * part + whole,
    )(q, g, zsum, state)
    zsum_grad = small_scan(local_zgrad, True)
    key_grad, value_grad = call(
        key_kernel, "key_value_grad", tokens, [TOKEN_BLOCK] * 2 + [STATE_BLOCK, ROW_BLOCK],
        [TOKEN_BLOCK] * 2, [token_out] * 2, 4 * work, 6 * part + whole,
    )(k, v, state_grad, zsum_grad)
    return tuple(a.reshape(1, tokens, WIDTH) for a in (query_grad, key_grad, value_grad))


def solution(mesh):
    placed = P("frame", "space", None)
    return jax.shard_map(
        on_device,
        mesh=mesh,
        in_specs=(placed,) * 4,
        out_specs=(placed,) * 3,
        check_vma=False,
    )
```
